32 devices in a mesh: grid: 8 (over z, y), layer: 4 (over x, core).
Axes of the slice: x: 2, y: 2, z: 4, core: 2. Of those that a mesh axis runs over, the one named last changes fastest.
Arguments:
- values: float32 [2048, 2048], P('grid', 'layer'), may hold values from 0.1 to 10
- occupancy: int32 [3, 16, 4], P(None, 'grid'), may hold values from 0 to 15, as said below
Outputs:
- flow_scaled: float32 [2048, 2048], P('grid', 'layer')
The draws below stay inside these ranges and needn't reach their ends.
Inputs may be any that keep to these rules, and one draw needn't show every extreme that they name: `occupancy`: each block row's list, in each of the 3 entries, names 4 distinct block columns, the row's own block column first.
All inputs are finite; a program needn't handle non-finite values.
Results may differ from the reference program's by a relative error of at most 0.00015.
Values sent between devices are 32-bit elements; how exact they have to be, the bound alone decides.
No kernel may reach another device: no remote copies, remote signals or barrier semaphores. Data moves between devices by JAX's collectives and lax.ppermute only.
A program may use at most 64 MiB of HBM per device.

```python
import math
import jax
import jax.numpy as jnp
from jax import lax

BLK = 128
ITERS = 2
NB = 16
N = 2048
OCC = 4


def draw_occupancy(key, part):

    def draw_list(row_key, row_id):
        others = jax.random.permutation(row_key, NB - 1).astype(jnp.int32)
        others = jnp.where(others >= row_id, others + 1, others)
        return jnp.concatenate([row_id[None], others[:OCC - 1]]).astype(jnp.int32)
    row_keys = jax.random.split(key, (ITERS + 1) * NB)
    row_ids = jnp.tile(jnp.arange(NB, dtype=jnp.int32), ITERS + 1)
    chosen = jax.vmap(draw_list)(row_keys, row_ids)
    return chosen.reshape(ITERS + 1, NB, OCC)


def levels(own_key, extent, cuts, least, top_value):
    loudness, own = 1.0, jax.random.fold_in(own_key, 6)
    for position, shards_of in cuts:
        steps = jnp.exp(jax.random.uniform(jax.random.fold_in(own, position), (shards_of,), jnp.float32, least / len(cuts), top_value / len(cuts)))
        loudness = loudness * jnp.repeat(steps, extent[position] // shards_of).reshape([-1 if axis == position else 1 for axis in range(len(extent))])
    return loudness


def setup_inputs(seed: int = 0) -> dict:
    key_list = jax.random.split(jax.random.key(seed), 3)
    values = jnp.clip(jnp.exp(math.log(10.0) - 4.6051702 * jax.random.uniform(key_list[0], (N, N), jnp.float32) ** levels(key_list[0], (N, N), ((0, 8), (1, 4)), -0.2, 0.2)), 0.1, 10.0)
    occupancy = draw_occupancy(jax.random.fold_in(key_list[2], 71), 0)
    return {"values": values, "occupancy": occupancy}


def block_mask(chosen):
    column_ids = jnp.arange(NB, dtype=jnp.int32)
    return jnp.any(chosen[:, :, None] == column_ids[None, None, :], axis=1).astype(jnp.float32)


def apply_mask(matrix, block_keep):
    shaped = matrix.reshape(NB, BLK, NB, BLK) * block_keep[:, None, :, None]
    return shaped.reshape(NB * BLK, NB * BLK)


def normalize(matrix):
    return matrix / jnp.sum(matrix, axis=0, keepdims=True)


def reference(values, occupancy):
    current = normalize(apply_mask(values, block_mask(occupancy[0])))
    for section in range(ITERS):
        product = jnp.dot(current, current, precision=lax.Precision.HIGHEST, preferred_element_type=jnp.float32)
        squared = apply_mask(product * product, block_mask(occupancy[section + 1]))
        current = normalize(squared)
    return current * (OCC * BLK)
```

```python
import functools

import jax
import jax.numpy as jnp
from jax import lax
from jax.experimental import pallas as pl
from jax.experimental.pallas import tpu as pltpu
from jax.sharding import PartitionSpec as P

BLK = 128
ITERS = 2
SUB = 8
AXES = ("grid", "layer")


class Shape:
    def __init__(self, grid, layer, rows_here, cols_here, occ):
        self.grid, self.layer, self.occ = grid, layer, occ
        self.z = 1
        while self.z * self.z < grid:
            self.z *= 2
        self.y = grid // self.z
        self.c = 2
        self.x = layer // self.c
        self.rows = rows_here // BLK
        self.cols = cols_here // BLK
        self.nb = self.rows * grid
        self.pairs = self.rows * occ
        self.mine = self.pairs // layer
        self.blocks = self.nb * occ

    def shift(self, dz=0, dy=0, dx=0, dc=0):
        out = []
        for g in range(self.grid):
            for l in range(self.layer):
                z, y, x, c = g // self.y, g % self.y, l // self.c, l % self.c
                z, y, x, c = (z + dz) % self.z, (y + dy) % self.y, (x + dx) % self.x, (c + dc) % self.c
                out.append((g * self.layer + l, (z * self.y + y) * self.layer + x * self.c + c))
        return out

    def here(self):
        g, l = lax.axis_index("grid"), lax.axis_index("layer")
        return g // self.y, g % self.y, l // self.c, l % self.c

    def send(self, array, **by):
        return lax.ppermute(array, AXES, self.shift(**by))


def compact(sh, values, occupancy):
    rows = sh.mine * BLK + SUB

    def kernel(lists, values_ref, lanes_ref, out_ref):
        _, _, x, c = sh.here()
        first = lax.axis_index("layer") * sh.cols
        for dc in range(sh.c):
            for dx in range(sh.x):
                layer = lax.rem(x + dx, sh.x) * sh.c + lax.rem(c + dc, sh.c)
                for p in range(sh.mine):
                    pair = layer * sh.mine + p
                    row = pair // sh.occ
                    column = lists[0, row, lax.rem(pair, sh.occ)] - first
                    held = jnp.logical_and(column >= 0, column < sh.cols)
                    at = jnp.clip(column, 0, sh.cols - 1)
                    block = values_ref[
                        pl.ds(pl.multiple_of(row * BLK, BLK), BLK), pl.ds(pl.multiple_of(at * BLK, BLK), BLK)
                    ]
                    out_ref[dc, dx, pl.ds(p * BLK, BLK), :] = jnp.where(held, block, 0.0)
                if dc == 0 and dx == 0:
                    out_ref[dc, dx, pl.ds(sh.mine * BLK, SUB), :] = lanes_ref[...]
                else:
                    out_ref[dc, dx, pl.ds(sh.mine * BLK, SUB), :] = jnp.zeros((SUB, BLK), jnp.float32)

    lanes = occupancy.reshape(ITERS + 1, sh.pairs).astype(jnp.float32)
    lanes = jnp.pad(lanes, ((0, SUB - ITERS - 1), (0, BLK - sh.pairs)))
    return pl.pallas_call(
        kernel,
        out_shape=jax.ShapeDtypeStruct((sh.c, sh.x, rows, BLK), jnp.float32),
        in_specs=[
            pl.BlockSpec(memory_space=pltpu.SMEM),
            pl.BlockSpec(memory_space=pltpu.VMEM),
            pl.BlockSpec(memory_space=pltpu.VMEM),
        ],
        out_specs=pl.BlockSpec(memory_space=pltpu.VMEM),
        name="compact",
    )(occupancy, values, lanes)


def balance(sh, parts):
    kept = parts[0]
    for dc in range(1, sh.c):
        kept = kept + sh.send(parts[dc], dc=dc)
    own = kept[0]
    for dx in range(1, sh.x):
        own = own + sh.send(kept[dx], dx=dx)
    return own


def split(block):
    high = block.astype(jnp.bfloat16)
    low = (block - high.astype(jnp.float32)).astype(jnp.bfloat16)
    return high, low


def tiles_sum(block):
    return jnp.sum(block.reshape(BLK // SUB, SUB, block.shape[-1]), axis=0)


def iterate_kernel(sh, pieces, *refs):
    inputs, (out_ref, lists_v, lists, place, chosen, high, low, squared, sums, sem) = refs[: len(pieces)], refs[len(pieces) :]
    z, y, x, c = sh.here()
    blocks, occ, nb, pairs, mine = sh.blocks, sh.occ, sh.nb, sh.pairs, sh.mine
    layer, grid = lax.axis_index("layer"), lax.axis_index("grid")

    def source(by):
        dz, dy, dx, dc = by
        g = lax.rem(z - dz + sh.z, sh.z) * sh.y + lax.rem(y - dy + sh.y, sh.y)
        l = lax.rem(x - dx + sh.x, sh.x) * sh.c + lax.rem(c - dc + sh.c, sh.c)
        return g, l

    def column(k, b):
        return lists[b // pairs, k, lax.rem(b, pairs)]

    for ref, piece in zip(inputs, pieces):
        for by, row, p in piece:
            if p is None and by[2:] == (0, 0):
                lists_v[source(by)[0]] = ref[pl.ds(row, SUB), :].astype(jnp.int32)
    copy = pltpu.make_async_copy(lists_v, lists, sem)
    copy.start()
    copy.wait()

    def every_block(do):
        for ref, piece in zip(inputs, pieces):
            for by, row, p in piece:
                if p is not None:
                    g, l = source(by)
                    do(g * pairs + l * mine + p, ref[pl.ds(row, BLK), :])

    def clear(n):
        sums[pl.ds(0, n)] = jnp.zeros((n, SUB, BLK), jnp.float32)

    def invert(n):
        total = jnp.sum(sums[pl.ds(0, n)], axis=1, keepdims=True)
        sums[pl.ds(0, n)] = jnp.broadcast_to(1.0 / total, (n, SUB, BLK))

    def put(b, block, inverse):
        scaled = (block.reshape(BLK // SUB, SUB, BLK) * inverse[None]).reshape(BLK, BLK)
        high[b], low[b] = split(scaled)

    def index_blocks(k):
        def none(i, _):
            place[i] = blocks
            return 0

        def one(b, _):
            place[(b // occ) * nb + column(k, b)] = b
            return 0

        lax.fori_loop(0, nb * nb, none, 0, unroll=8)
        lax.fori_loop(0, blocks, one, 0, unroll=4)

    def rows_of(r):
        h = [high[r * occ + s] for s in range(occ)]
        l = [low[r * occ + s] for s in range(occ)]
        return jnp.concatenate(h + h + l, axis=1)

    def columns_of(k, r, wanted):
        stacks = []
        for col in wanted:
            at = [place[column(k, r * occ + s) * nb + col] for s in range(occ)]
            h = [high[i] for i in at]
            stacks.append(jnp.concatenate(h + [low[i] for i in at] + h, axis=0))
        return jnp.concatenate(stacks, axis=1)

    def dot(a, b):
        return lax.dot(a, b, preferred_element_type=jnp.float32)

    clear(nb)

    def add_start(b, block):
        col = column(0, b)
        sums[col] += tiles_sum(block)

    every_block(add_start)
    invert(nb)
    every_block(lambda b, block: put(b, block, sums[column(0, b)]))
    high[blocks] = jnp.zeros((BLK, BLK), jnp.bfloat16)
    low[blocks] = jnp.zeros((BLK, BLK), jnp.bfloat16)
    index_blocks(0)

    clear(nb)
    width = min(occ, 4)

    def first(i, _):
        r, t0 = i // (occ // width), lax.rem(i, occ // width) * width
        wanted = [column(1, r * occ + t0 + t) for t in range(width)]
        product = dot(rows_of(r), columns_of(0, r, wanted))
        product = product * product
        for t in range(width):
            block = product[:, t * BLK : (t + 1) * BLK]
            squared[r * occ + t0 + t] = block
            sums[wanted[t]] += tiles_sum(block)
        return 0

    lax.fori_loop(0, nb * (occ // width), first, 0)
    invert(nb)

    def renew(b, _):
        put(b, squared[b], sums[column(1, b)])
        return 0

    lax.fori_loop(0, blocks, renew, 0, unroll=2)
    index_blocks(1)

    clear(sh.cols)

    def list_own(b, n):
        chosen[n] = b
        return n + (column(2, b) // sh.cols == layer).astype(jnp.int32)

    count = lax.fori_loop(0, blocks, list_own, 0, unroll=4)

    def second(i, _):
        b = chosen[i]
        col = column(2, b)
        product = dot(rows_of(b // occ), columns_of(1, b // occ, [col]))
        product = product * product
        squared[b] = product
        sums[col - layer * sh.cols] += tiles_sum(product)
        return 0

    lax.fori_loop(0, count, second, 0)
    invert(sh.cols)
    out_ref[...] = jnp.zeros(out_ref.shape, jnp.float32)
    for q in range(pairs):
        b = grid * pairs + q
        col = column(2, b) - layer * sh.cols

        @pl.when(jnp.logical_and(col >= 0, col < sh.cols))
        def _():
            scale = sums[col] * float(occ * BLK)
            block = (squared[b].reshape(BLK // SUB, SUB, BLK) * scale[None]).reshape(BLK, BLK)
            out_ref[pl.ds((q // occ) * BLK, BLK), pl.ds(pl.multiple_of(col * BLK, BLK), BLK)] = block


def iterate(sh, arrays, pieces):
    return pl.pallas_call(
        functools.partial(iterate_kernel, sh, pieces),
        out_shape=jax.ShapeDtypeStruct((sh.rows * BLK, sh.cols * BLK), jnp.float32),
        in_specs=[pl.BlockSpec(memory_space=pltpu.VMEM)] * len(arrays),
        out_specs=pl.BlockSpec(memory_space=pltpu.VMEM),
        scratch_shapes=[
            pltpu.VMEM((sh.grid, SUB, BLK), jnp.int32),
            pltpu.SMEM((sh.grid, SUB, BLK), jnp.int32),
            pltpu.SMEM((sh.nb * sh.nb,), jnp.int32),
            pltpu.SMEM((sh.blocks + 1,), jnp.int32),
            pltpu.VMEM((sh.blocks + 1, BLK, BLK), jnp.bfloat16),
            pltpu.VMEM((sh.blocks + 1, BLK, BLK), jnp.bfloat16),
            pltpu.VMEM((sh.blocks, BLK, BLK), jnp.float32),
            pltpu.VMEM((sh.nb, SUB, BLK), jnp.float32),
            pltpu.SemaphoreType.DMA,
        ],
        name="iterate",
    )(*arrays)


def gather_general(sh, own):
    rows = own.shape[0]
    everything = lax.all_gather(own, AXES, axis=0, tiled=True)
    z, y, x, c = sh.here()
    shaped = everything.reshape(sh.z, sh.y, sh.x, sh.c, rows, BLK)
    for axis, at in enumerate((z, y, x, c)):
        shaped = jnp.roll(shaped, -at, axis=axis)
    piece = []
    n = 0
    for dz in range(sh.z):
        for dy in range(sh.y):
            for dx in range(sh.x):
                for dc in range(sh.c):
                    by = (-dz % sh.z, -dy % sh.y, -dx % sh.x, -dc % sh.c)
                    piece += [(by, n + p * BLK, p) for p in range(sh.mine)]
                    piece += [(by, n + sh.mine * BLK, None)]
                    n += rows
    return [shaped.reshape(n, BLK)], [piece]


def gather_torus(sh, own):
    half = sh.mine // 2 * BLK
    base = [(p * BLK, p) for p in range(sh.mine)] + [(sh.mine * BLK, None)]
    arrays, pieces = [], []

    def add(array, piece):
        arrays.append(array)
        pieces.append(piece)
        moved = [((b[0], b[1], b[2], (b[3] + 1) % sh.c), row, p) for b, row, p in piece]
        arrays.append(sh.send(array, dc=1))
        pieces.append(moved)

    def hop(array, piece, axis):
        by = {"dy" if axis == 1 else "dx": 1}
        n = (sh.y, sh.x)[axis - 1]
        moved = [(b[:axis] + ((b[axis] + 1) % n,) + b[axis + 1 :], row, p) for b, row, p in piece]
        return sh.send(array, **by), moved

    along_z = [sh.send(own, dz=dz) for dz in range(1, sh.z)]
    piece = [((0, 0, 0, 0), row, p) for row, p in base]
    add(own, piece)
    y1 = hop(own, piece, 1)
    x1 = hop(own, piece, 2)
    diagonal = [((0, 1, 1, 0), row, p) for row, p in base]
    xy = sh.send(own, dy=1, dx=1), diagonal
    add(*y1), add(*x1), add(*xy)
    for lo, hi, order in ((0, half, (1, 2)), (half, sh.mine * BLK + SUB, (2, 1))):
        stack, piece = jnp.concatenate([a[lo:hi] for a in along_z], axis=0), []
        for dz in range(1, sh.z):
            for row, p in base:
                if lo <= row < hi:
                    piece.append(((dz, 0, 0, 0), row - lo + (dz - 1) * (hi - lo), p))
        one = hop(stack, piece, order[0])
        two = hop(stack, piece, order[1])
        both = hop(*one, order[1])
        add(stack, piece), add(*one), add(*two), add(*both)
    return arrays, pieces


def local(grid, layer, values, occupancy):
    sh = Shape(grid, layer, values.shape[0], values.shape[1], occupancy.shape[2])
    own = balance(sh, compact(sh, values, occupancy))
    if (sh.y, sh.x) == (2, 2) and sh.mine % 2 == 0:
        arrays, pieces = gather_torus(sh, own)
    else:
        arrays, pieces = gather_general(sh, own)
    return iterate(sh, arrays, pieces)


def solution(mesh):
    return jax.shard_map(
        functools.partial(local, mesh.shape["grid"], mesh.shape["layer"]),
        mesh=mesh,
        in_specs=(P("grid", "layer"), P(None, "grid", None)),
        out_specs=P("grid", "layer"),
        check_vma=False,
    )
```
